32 devices in a mesh: mem: 8 (over y, x, core), patch: 4 (over z).
Axes of the slice: x: 2, y: 2, z: 4, core: 2. Of those that a mesh axis runs over, the one named last changes fastest.
Arguments:
- ens: bfloat16 [2, 256, 8, 4096], P(None, 'mem', None, 'patch'), may hold values from -6 to 6
- obs_pert: bfloat16 [2, 256, 2048], P(None, None, 'patch'), may hold values from -6 to 6
- obs_innov: bfloat16 [2, 2048], P(None, 'patch'), may hold values from -6 to 6
- obs_pos: bfloat16 [2, 2048], P(None, 'patch'), may hold values from 0 to 1
- obs_prec: bfloat16 [2, 2048], P(None, 'patch'), may hold values from 0.25 to 4
Outputs:
- analysed: bfloat16 [2, 256, 8, 4096], P(None, 'mem', None, 'patch')
The draws below stay inside these ranges and needn't reach their ends.
All inputs are finite; a program needn't handle non-finite values.
Results may differ from the reference program's by a relative error of at most 0.0058.
Values may be sent and summed in bfloat16 or wider, within the bound.
A program may use at most 64 MiB of HBM per device.

```python
import math
import jax
import jax.numpy as jnp
from jax import lax

K = 256
SLABS = 2
LEVELS = 8
GSUB = 128
NOB_DEV = 512
NS_ITERS = 2
GCOL = 4096
NOBS = 2048
N_MEM = 8
N_PATCH = 4


def block_scale(stream_key, shape, pieces, least, high):
    factor_of = 1.0
    for dim, parts in pieces:
        draws = jax.random.uniform(jax.random.fold_in(jax.random.fold_in(stream_key, 6), dim), (parts,), jnp.float32, least / len(pieces), high / len(pieces))
        factor_of = factor_of * jnp.repeat(jnp.exp(draws), shape[dim] // parts).reshape((-1,) + (1,) * (len(shape) - 1 - dim))
    return factor_of


def noise(stream_key, shape, width, reach, split=(), held_as=jnp.bfloat16):
    values = jax.random.normal(stream_key, shape, jnp.float32) * width
    if len(split) > 0:
        values = block_scale(stream_key, shape, split, -0.22, 0.18) * values
    return jnp.clip(values, min=-reach, max=reach).astype(held_as)


def setup_inputs(seed: int = 0) -> dict:
    splits = jax.random.split(jax.random.key(seed), 6)
    return {
        "ens": noise(splits[0], (SLABS, K, LEVELS, GCOL), 1.0, 6.0, ((1, 8), (3, 4))),
        "obs_pert": noise(splits[1], (SLABS, K, NOBS), 1.0, 6.0, ((2, 4),)),
        "obs_innov": noise(splits[2], (SLABS, NOBS), 1.0, 6.0, ((1, 4),)),
        "obs_pos": jnp.clip(1.0 * jax.random.uniform(splits[3], (SLABS, NOBS), jnp.float32) ** block_scale(splits[3], (SLABS, NOBS), ((1, 4),), -0.2, 0.2), 0.0, 1.0).astype(jnp.bfloat16),
        "obs_prec": jnp.clip(jnp.exp(math.log(4.0) - 2.7725887 * jax.random.uniform(splits[4], (SLABS, NOBS), jnp.float32) ** block_scale(splits[4], (SLABS, NOBS), ((1, 4),), -0.2, 0.2)), 0.25, 4.0).astype(jnp.bfloat16),
    }


loc_scale = 0.5

def matmul(left, right):
    return jnp.dot(left, right, precision=lax.Precision.HIGHEST)

def region_weights(deviations, innovation, position, precision, center):
    members = deviations.shape[0]
    taper = jnp.exp(-0.5 * ((position - center) / loc_scale) ** 2)
    obs_weight = taper * precision.astype(jnp.float32)
    scaled = (deviations.astype(jnp.float32) * obs_weight[None, :]).astype(jnp.bfloat16)
    gram_sum = jnp.dot(scaled, deviations.T, preferred_element_type=jnp.float32)
    innov_sum = jnp.dot(scaled, innovation, preferred_element_type=jnp.float32)
    identity = jnp.eye(members, dtype=jnp.float32)
    system = (members - 1.0) * identity + gram_sum
    frobenius = jnp.sqrt(jnp.sum(system * system))
    current = system / frobenius
    inverse = identity
    for sweep in range(NS_ITERS):
        factor = 1.5 * identity - 0.5 * matmul(inverse, current)
        if sweep + 1 < NS_ITERS:
            current = matmul(current, factor)
        inverse = matmul(factor, inverse)
    inner = jnp.dot(inverse, innov_sum, precision=lax.Precision.HIGHEST)
    mean_weight = jnp.dot(inverse, inner, precision=lax.Precision.HIGHEST) / frobenius
    spread = inverse * jnp.sqrt((members - 1.0) / frobenius)
    return (spread + mean_weight[:, None]).astype(jnp.bfloat16)

def three_patches(values, axis):
    return jnp.concatenate([jnp.roll(values, 1, axis=axis), values, jnp.roll(values, -1, axis=axis)], axis=-1)

def reference(ens, obs_pert, obs_innov, obs_pos, obs_prec):
    members = obs_pert.shape[1]
    slab_count = ens.shape[0]
    level_count = ens.shape[2]
    deviations = three_patches(obs_pert.reshape(slab_count, members, N_PATCH, NOB_DEV), 2)
    deviations = deviations.transpose(0, 2, 1, 3).reshape(slab_count * N_PATCH, members, 3 * NOB_DEV)
    innovation = three_patches(obs_innov.reshape(slab_count, N_PATCH, NOB_DEV), 1).reshape(slab_count * N_PATCH, 3 * NOB_DEV)
    offsets = jnp.repeat(jnp.array([-1.0, 0.0, 1.0], jnp.float32), NOB_DEV)
    position = three_patches(obs_pos.astype(jnp.float32).reshape(slab_count, N_PATCH, NOB_DEV), 1) + offsets
    position = position.reshape(slab_count * N_PATCH, 3 * NOB_DEV)
    precision = three_patches(obs_prec.reshape(slab_count, N_PATCH, NOB_DEV), 1).reshape(slab_count * N_PATCH, 3 * NOB_DEV)
    centers = (jnp.arange(N_MEM, dtype=jnp.float32) + 0.5) / N_MEM

    def one_patch(items):
        dev_rows, innov_row, pos_row, prec_row = items
        return jax.vmap(lambda center: region_weights(dev_rows, innov_row, pos_row, prec_row, center))(centers)
    weights = lax.map(one_patch, (deviations, innovation, position, precision))
    weights = weights.reshape(slab_count, N_PATCH, N_MEM, members, members).transpose(1, 0, 2, 3, 4)
    blocks = ens.reshape(slab_count, members, level_count, N_PATCH, N_MEM, GSUB).transpose(3, 0, 1, 2, 4, 5)

    def apply_patch(items):
        block, wts = items
        average = lax.optimization_barrier(jnp.mean(block.astype(jnp.float32), axis=1, keepdims=True))
        anomaly = (block.astype(jnp.float32) - average).astype(jnp.bfloat16)
        mixed = jnp.einsum('sjlmg,smjk->sklmg', anomaly.astype(jnp.float32), wts.astype(jnp.float32))
        return (average + mixed).astype(jnp.bfloat16)
    result = lax.map(apply_patch, (blocks, weights))
    return result.transpose(1, 2, 3, 0, 4, 5).reshape(slab_count, members, level_count, N_PATCH * N_MEM * GSUB)
```

```python
import functools
import jax
import jax.numpy as jnp
from jax import lax
from jax.experimental import pallas as pl
from jax.experimental.pallas import tpu as pltpu
from jax.sharding import PartitionSpec as P

loc_scale = 0.5
MESH = pl.DeviceIdType.MESH
F32 = jnp.float32
BF16 = jnp.bfloat16
NT = (((1,), (1,)), ((), ()))


def split(x):
    high = x.astype(BF16)
    return high, (x - high.astype(F32)).astype(BF16)


def mm(a, b):
    return jnp.dot(a, b, preferred_element_type=F32)


def mm3(a, b):
    return mm(a[0], b[0]) + (mm(a[0], b[1]) + mm(a[1], b[0]))


def peer_of(me, step, count):
    if count & (count - 1):
        return lax.rem(me + step, count)
    bit, peer = 1, 0
    while bit < count:
        mine = lax.rem(me // bit, 2)
        peer = peer + bit * ((1 - mine) if step & bit else mine)
        bit *= 2
    return peer


def kernel(
    n, patches, ens, pert, innov, pos, prec, out,
    xin, ybuf, own, near, small, small_near, gram, rhs, anom, abf, wide,
    local_sem, keep_sem, in_send, in_recv, out_send, out_recv, back_sem,
    z_send, z_recv, s_send, s_recv, f_send, f_recv, ready,
):
    slabs, mloc, levels, _ = ens.shape
    members, nob = pert.shape[1], pert.shape[2]
    group = ens.shape[3] // n
    half = members // 2
    me = lax.axis_index("mem")
    patch = lax.axis_index("patch")
    core = lax.rem(me, 2)
    partner = me + 1 - 2 * core
    up = lax.rem(patch + 1, patches)
    down = lax.rem(patch + patches - 1, patches)
    steps = sorted(range(1, n), key=lambda d: (-bin(d // 2).count("1"), d % 2, d))
    peers = [peer_of(me, d, n) for d in steps]

    load_pert = pltpu.make_async_copy(pert, own, local_sem.at[1])
    load_small = [
        pltpu.make_async_copy(ref, small.at[i], local_sem.at[2 + i])
        for i, ref in enumerate((innov, pos, prec))
    ]
    load_pert.start()
    for c in load_small:
        c.start()

    def rows(q):
        return pl.ds(pl.multiple_of(q * mloc, mloc), mloc)

    def cols(q):
        return pl.ds(pl.multiple_of(q * group, group), group)

    keep = []
    for s in range(slabs):
        c = pltpu.make_async_copy(ens.at[s, :, :, cols(me)], xin.at[s, rows(me)], keep_sem.at[s])
        c.start()
        keep.append(c)

    barrier = pltpu.get_barrier_semaphore()
    for q in peers:
        pl.semaphore_signal(barrier, inc=1, device_id=(q, patch), device_id_type=MESH)
    for z in (up, down):
        @pl.when(z > patch)
        def _():
            pl.semaphore_signal(barrier, inc=1, device_id=(me, z), device_id_type=MESH)
    lower = (up < patch).astype(jnp.int32) + (down < patch).astype(jnp.int32)
    pl.semaphore_wait(barrier, len(peers) + lower)

    mine = pl.ds(pl.multiple_of(core * half, half), half)
    sends = []
    small_copies = []
    zc = {}
    targets = (up, down)

    def send_ens(s, some):
        for q in some:
            pltpu.make_async_remote_copy(
                ens.at[s, :, :, cols(q)], xin.at[s, rows(me)], in_send.at[s], in_recv.at[s],
                device_id=(q, patch), device_id_type=MESH).start()

    for d, z in enumerate(targets):
        @pl.when(z < patch)
        def _():
            pl.semaphore_signal(ready.at[1 - d], inc=1, device_id=(me, z), device_id_type=MESH)
    for d in (0, 1):
        small_copies.append(pltpu.make_async_remote_copy(
            small, small_near.at[d], s_send.at[d], s_recv.at[d],
            device_id=(me, targets[d]), device_id_type=MESH))
        for s in range(slabs):
            zc[d, s] = pltpu.make_async_remote_copy(
                own.at[s, mine], near.at[d, s, mine], z_send.at[d, s], z_recv.at[d, s],
                device_id=(me, targets[d]), device_id_type=MESH)
            sends.append(zc[d, s])

    send_ens(0, peers)
    for c in load_small:
        c.wait()
    load_pert.wait()
    for d, z in enumerate(targets):
        @pl.when(z < patch)
        def _():
            small_copies[d].start()
            zc[d, 0].start()
    for d, z in enumerate(targets):
        @pl.when(z > patch)
        def _():
            pl.semaphore_wait(ready.at[d], 1)
            small_copies[d].start()
            zc[d, 0].start()
    for s in range(1, slabs):
        for d in (0, 1):
            zc[d, s].start()
        send_ens(s, peers)

    center = (me.astype(F32) + 0.5) / n

    def accumulate(s, dev_ref, small_ref, offset, first):
        vals = small_ref[...].astype(F32)
        distance = vals[1] + offset - center
        taper = jnp.exp(-0.5 * (distance / loc_scale) ** 2)
        weight = taper * vals[2]
        dev = dev_ref[...]
        scaled = (dev.astype(F32) * weight[s:s + 1, :]).astype(BF16)
        row = jnp.broadcast_to(vals[0][s:s + 1, :], (16, nob)).astype(BF16)
        both = lax.dot_general(
            jnp.concatenate([dev, row], axis=0), scaled, NT, preferred_element_type=F32)
        g, r = both[:members], both[members:]
        if first:
            gram[s] = g
            rhs[s] = r
        else:
            gram[s] += g
            rhs[s] += r

    for s in range(slabs):
        accumulate(s, own.at[s], small, 0.0, True)

    fwd = {}

    def relay(s):
        for d in (0, 1):
            zc[d, s].wait_recv()
            c = pltpu.make_async_remote_copy(
                near.at[d, s, mine], near.at[d, s, mine], f_send.at[d, s], f_recv.at[d, s],
                device_id=(partner, patch), device_id_type=MESH)
            c.start()
            fwd[d, s] = c

    def weights_of(s):
        diag = (
            lax.broadcasted_iota(jnp.int32, (members, members), 0)
            == lax.broadcasted_iota(jnp.int32, (members, members), 1)
        )
        system = gram[s] + jnp.where(diag, members - 1.0, 0.0)
        parts = split(system)
        fro2 = jnp.sum(jnp.sum(system * system, axis=0, keepdims=True), axis=1, keepdims=True)
        inv_fro = 1.0 / jnp.sqrt(fro2)
        cur = system * inv_fro
        cur2 = mm3(parts, parts) * (inv_fro * inv_fro)
        tail = 0.0625 * cur2 - 0.5625 * cur
        inverse = (
            jnp.where(diag, 2.25, 0.0) - 2.4375 * cur + 1.6875 * cur2
            + mm(cur2.astype(BF16), tail.astype(BF16))
        )
        inner = jnp.sum(inverse * rhs[s, 0:1, :], axis=1, keepdims=True)
        mean_weight = jnp.sum(inverse * inner, axis=0, keepdims=True) * inv_fro
        spread = inverse * jnp.sqrt((members - 1.0) * inv_fro)
        return (spread + mean_weight).astype(BF16)

    def centre(s):
        x = xin[s].astype(F32)
        average = jnp.sum(x, axis=0) * (1.0 / members)
        anom[...] = (x - average[None]).reshape(members * levels, group)
        for l in range(levels):
            abf[:, l * group:(l + 1) * group] = anom[pl.ds(l, members, stride=levels), :].astype(BF16)
        return average

    def apply(s, average, w):
        wide[...] = w
        parts = 1 if n & (n - 1) else 2
        size = members // parts
        for part in range(parts):
            block = (1 - part + (2 * part - 1) * (me // (n // 2))) if parts == 2 else 0
            base = pl.multiple_of(block * size, size)
            start = part * size * levels
            wp = wide[pl.ds(base, size), :]
            for l in range(0, levels, 2):
                mixed = mm(wp, abf[:, l * group:(l + 2) * group])
                anom[pl.ds(start + l, size, stride=levels), :] = mixed[:, :group]
                anom[pl.ds(start + l + 1, size, stride=levels), :] = mixed[:, group:]
            x = anom[pl.ds(start, size * levels), :].reshape(size, levels, group) + average[None]
            ybuf[s, pl.ds(base, size)] = x.astype(BF16)
            for d, q in zip(steps, peers):
                if parts == 1 or (d >= n // 2) == (part == 0):
                    pltpu.make_async_remote_copy(
                        ybuf.at[s, rows(q)], out.at[s, :, :, cols(me)], out_send.at[s],
                        out_recv.at[s], device_id=(q, patch), device_id_type=MESH).start()

    back = []
    others = (n - 1) * mloc

    def arrived(s):
        pltpu.make_async_copy(
            xin.at[s, pl.ds(0, others)], xin.at[s, pl.ds(0, others)], in_recv.at[s]).wait()

    for s in range(slabs):
        if s == 0:
            for c in small_copies:
                c.wait_recv()
        relay(s)
        keep[s].wait()
        arrived(s)
        average = centre(s)
        for d, offset in ((0, -1.0), (1, 1.0)):
            fwd[d, s].wait_recv()
            accumulate(s, near.at[d, s], small_near.at[d], offset, False)
        w = weights_of(s)
        apply(s, average, w)
        c = pltpu.make_async_copy(ybuf.at[s, rows(me)], out.at[s, :, :, cols(me)], back_sem.at[s])
        c.start()
        back.append(c)

    for c in sends + small_copies:
        c.wait_send()
    for c in fwd.values():
        c.wait_send()
    for s in range(slabs):
        back[s].wait()
        for sem in (in_send, out_send, out_recv):
            pltpu.make_async_copy(
                xin.at[s, pl.ds(0, others)], xin.at[s, pl.ds(0, others)], sem.at[s]).wait()


def solution(mesh):
    n, patches = mesh.shape["mem"], mesh.shape["patch"]

    def on_device(ens, obs_pert, obs_innov, obs_pos, obs_prec):
        slabs, mloc, levels, width = ens.shape
        members, nob = obs_pert.shape[1:]
        group = width // n
        DMA = pltpu.SemaphoreType.DMA
        return pl.pallas_call(
            functools.partial(kernel, n, patches),
            out_shape=pltpu.VMEM(ens.shape, ens.dtype),
            in_specs=[pl.BlockSpec(memory_space=pltpu.HBM)] * 5,
            out_specs=pl.BlockSpec(memory_space=pltpu.VMEM),
            scratch_shapes=[
                pltpu.VMEM((slabs, members, levels, group), BF16),
                pltpu.VMEM((slabs, members, levels, group), BF16),
                pltpu.VMEM((slabs, members, nob), BF16),
                pltpu.VMEM((2, slabs, members, nob), BF16),
                pltpu.VMEM((3, slabs, nob), BF16),
                pltpu.VMEM((2, 3, slabs, nob), BF16),
                pltpu.VMEM((slabs, members, members), F32),
                pltpu.VMEM((slabs, 16, members), F32),
                pltpu.VMEM((members * levels, group), F32),
                pltpu.VMEM((members, levels * group), BF16),
                pltpu.VMEM((members, members), BF16),
                DMA((5,)), DMA((slabs,)),
                DMA((slabs,)), DMA((slabs,)), DMA((slabs,)), DMA((slabs,)), DMA((slabs,)),
                DMA((2, slabs)), DMA((2, slabs)), DMA((2,)), DMA((2,)),
                DMA((2, slabs)), DMA((2, slabs)), pltpu.SemaphoreType.REGULAR((2,)),
            ],
            compiler_params=pltpu.CompilerParams(
                collective_id=0, has_side_effects=True, vmem_limit_bytes=50000000),
        )(*[pltpu.with_memory_space_constraint(a, pltpu.HBM) for a in (ens, obs_pert, obs_innov, obs_pos, obs_prec)])

    placed = (
        P(None, "mem", None, "patch"),
        P(None, None, "patch"),
        P(None, "patch"),
        P(None, "patch"),
        P(None, "patch"),
    )
    return jax.shard_map(
        on_device,
        mesh=mesh,
        in_specs=placed,
        out_specs=P(None, "mem", None, "patch"),
        check_vma=False,
    )
```

```python
import functools
import jax
import jax.numpy as jnp
from jax import lax
from jax.experimental import pallas as pl
from jax.experimental.pallas import tpu as pltpu
from jax.sharding import PartitionSpec as P

loc_scale = 0.5
MESH = pl.DeviceIdType.MESH
F32 = jnp.float32
BF16 = jnp.bfloat16
NT = (((1,), (1,)), ((), ()))


def split(x):
    high = x.astype(BF16)
    return high, (x - high.astype(F32)).astype(BF16)


def mm(a, b):
    return jnp.dot(a, b, preferred_element_type=F32)


def mm3(a, b):
    return mm(a[0], b[0]) + (mm(a[0], b[1]) + mm(a[1], b[0]))


def peer_of(me, step, count):
    if count & (count - 1):
        return lax.rem(me + step, count)
    bit, peer = 1, 0
    while bit < count:
        mine = lax.rem(me // bit, 2)
        peer = peer + bit * ((1 - mine) if step & bit else mine)
        bit *= 2
    return peer


def kernel(
    n, patches, ens, pert, innov, pos, prec, out,
    xin, ybuf, own, near, small, small_near, gram, rhs, anom, abf, wide,
    local_sem, keep_sem, in_send, in_recv, out_send, out_recv, back_sem,
    z_send, z_recv, s_send, s_recv, f_send, f_recv, ready,
):
    slabs, mloc, levels, _ = ens.shape
    members, nob = pert.shape[1], pert.shape[2]
    group = ens.shape[3] // n
    half = members // 2
    me = lax.axis_index("mem")
    patch = lax.axis_index("patch")
    core = lax.rem(me, 2)
    partner = me + 1 - 2 * core
    up = lax.rem(patch + 1, patches)
    down = lax.rem(patch + patches - 1, patches)
    steps = sorted(range(1, n), key=lambda d: (d < 2, d % 2, bin(d // 2).count("1"), d))
    peers = [peer_of(me, d, n) for d in steps]

    barrier = pltpu.get_barrier_semaphore()
    for q in peers:
        pl.semaphore_signal(barrier, inc=1, device_id=(q, patch), device_id_type=MESH)
    for z in (up, down):
        @pl.when(z > patch)
        def _():
            pl.semaphore_signal(barrier, inc=1, device_id=(me, z), device_id_type=MESH)

    load_pert = pltpu.make_async_copy(pert, own, local_sem.at[1])
    load_small = [
        pltpu.make_async_copy(ref, small.at[i], local_sem.at[2 + i])
        for i, ref in enumerate((innov, pos, prec))
    ]
    for c in load_small:
        c.start()

    def rows(q):
        return pl.ds(pl.multiple_of(q * mloc, mloc), mloc)

    def cols(q):
        return pl.ds(pl.multiple_of(q * group, group), group)

    keep = []
    for s in range(slabs):
        c = pltpu.make_async_copy(ens.at[s, :, :, cols(me)], xin.at[s, rows(me)], keep_sem.at[s])
        keep.append(c)

    lower = (up < patch).astype(jnp.int32) + (down < patch).astype(jnp.int32)
    pl.semaphore_wait(barrier, len(peers) + lower)

    mine = pl.ds(pl.multiple_of(core * half, half), half)
    sends = []
    small_copies = []
    zc = {}
    targets = (up, down)

    def send_ens(s, some):
        for q in some:
            pltpu.make_async_remote_copy(
                ens.at[s, :, :, cols(q)], xin.at[s, rows(me)], in_send.at[s], in_recv.at[s],
                device_id=(q, patch), device_id_type=MESH).start()

    for d, z in enumerate(targets):
        @pl.when(z < patch)
        def _():
            pl.semaphore_signal(ready.at[1 - d], inc=1, device_id=(me, z), device_id_type=MESH)
    for d in (0, 1):
        small_copies.append(pltpu.make_async_remote_copy(
            small, small_near.at[d], s_send.at[d], s_recv.at[d],
            device_id=(me, targets[d]), device_id_type=MESH))
        for s in range(slabs):
            zc[d, s] = pltpu.make_async_remote_copy(
                pert.at[s, mine], near.at[d, s, mine], z_send.at[d, s], z_recv.at[d, s],
                device_id=(me, targets[d]), device_id_type=MESH)
            sends.append(zc[d, s])

    send_ens(0, peers)
    load_pert.start()
    for c in keep:
        c.start()
    for c in load_small:
        c.wait()
    for d, z in enumerate(targets):
        @pl.when(z < patch)
        def _():
            small_copies[d].start()
            zc[d, 0].start()
    for d, z in enumerate(targets):
        @pl.when(z > patch)
        def _():
            pl.semaphore_wait(ready.at[d], 1)
            small_copies[d].start()
            zc[d, 0].start()
    for s in range(1, slabs):
        for d in (0, 1):
            zc[d, s].start()
        send_ens(s, peers)

    load_pert.wait()
    center = (me.astype(F32) + 0.5) / n

    def accumulate(s, dev_ref, small_ref, offset, first):
        vals = small_ref[...].astype(F32)
        distance = vals[1] + offset - center
        taper = jnp.exp(-0.5 * (distance / loc_scale) ** 2)
        weight = taper * vals[2]
        dev = dev_ref[...]
        scaled = (dev.astype(F32) * weight[s:s + 1, :]).astype(BF16)
        row = jnp.broadcast_to(vals[0][s:s + 1, :], (16, nob)).astype(BF16)
        both = lax.dot_general(
            jnp.concatenate([dev, row], axis=0), scaled, NT, preferred_element_type=F32)
        g, r = both[:members], both[members:]
        if first:
            gram[s] = g
            rhs[s] = r
        else:
            gram[s] += g
            rhs[s] += r

    for s in range(slabs):
        accumulate(s, own.at[s], small, 0.0, True)

    fwd = {}

    def relay(s):
        for d in (0, 1):
            zc[d, s].wait_recv()
            c = pltpu.make_async_remote_copy(
                near.at[d, s, mine], near.at[d, s, mine], f_send.at[d, s], f_recv.at[d, s],
                device_id=(partner, patch), device_id_type=MESH)
            c.start()
            fwd[d, s] = c

    def weights_of(s):
        diag = (
            lax.broadcasted_iota(jnp.int32, (members, members), 0)
            == lax.broadcasted_iota(jnp.int32, (members, members), 1)
        )
        system = gram[s] + jnp.where(diag, members - 1.0, 0.0)
        parts = split(system)
        fro2 = jnp.sum(jnp.sum(system * system, axis=0, keepdims=True), axis=1, keepdims=True)
        inv_fro = 1.0 / jnp.sqrt(fro2)
        cur = system * inv_fro
        cur2 = mm3(parts, parts) * (inv_fro * inv_fro)
        tail = 0.0625 * cur2 - 0.5625 * cur
        inverse = (
            jnp.where(diag, 2.25, 0.0) - 2.4375 * cur + 1.6875 * cur2
            + mm(cur2.astype(BF16), tail.astype(BF16))
        )
        inner = jnp.sum(inverse * rhs[s, 0:1, :], axis=1, keepdims=True)
        mean_weight = jnp.sum(inverse * inner, axis=0, keepdims=True) * inv_fro
        spread = inverse * jnp.sqrt((members - 1.0) * inv_fro)
        return (spread + mean_weight).astype(BF16)

    def centre(s):
        x = xin[s].astype(F32)
        average = jnp.sum(x, axis=0) * (1.0 / members)
        anom[...] = (x - average[None]).reshape(members * levels, group)
        for l in range(levels):
            abf[:, l * group:(l + 1) * group] = anom[pl.ds(l, members, stride=levels), :].astype(BF16)
        return average

    def apply(s, average, w):
        wide[...] = w
        parts = 1 if n & (n - 1) else 2
        size = members // parts
        for part in range(parts):
            block = (1 - part + (2 * part - 1) * (me // (n // 2))) if parts == 2 else 0
            base = pl.multiple_of(block * size, size)
            start = part * size * levels
            wp = wide[pl.ds(base, size), :]
            for l in range(0, levels, 2):
                mixed = mm(wp, abf[:, l * group:(l + 2) * group])
                anom[pl.ds(start + l, size, stride=levels), :] = mixed[:, :group]
                anom[pl.ds(start + l + 1, size, stride=levels), :] = mixed[:, group:]
            x = anom[pl.ds(start, size * levels), :].reshape(size, levels, group) + average[None]
            ybuf[s, pl.ds(base, size)] = x.astype(BF16)
            for d, q in zip(steps, peers):
                if parts == 1 or (d >= n // 2) == (part == 0):
                    pltpu.make_async_remote_copy(
                        ybuf.at[s, rows(q)], out.at[s, :, :, cols(me)], out_send.at[s],
                        out_recv.at[s], device_id=(q, patch), device_id_type=MESH).start()

    back = []
    others = (n - 1) * mloc

    def arrived(s):
        pltpu.make_async_copy(
            xin.at[s, pl.ds(0, others)], xin.at[s, pl.ds(0, others)], in_recv.at[s]).wait()

    for s in range(slabs):
        if s == 0:
            for c in small_copies:
                c.wait_recv()
        relay(s)
        keep[s].wait()
        arrived(s)
        average = centre(s)
        for d, offset in ((0, -1.0), (1, 1.0)):
            fwd[d, s].wait_recv()
            accumulate(s, near.at[d, s], small_near.at[d], offset, False)
        w = weights_of(s)
        apply(s, average, w)
        c = pltpu.make_async_copy(ybuf.at[s, rows(me)], out.at[s, :, :, cols(me)], back_sem.at[s])
        c.start()
        back.append(c)

    for c in sends + small_copies:
        c.wait_send()
    for c in fwd.values():
        c.wait_send()
    for s in range(slabs):
        back[s].wait()
        for sem in (in_send, out_send, out_recv):
            pltpu.make_async_copy(
                xin.at[s, pl.ds(0, others)], xin.at[s, pl.ds(0, others)], sem.at[s]).wait()


def solution(mesh):
    n, patches = mesh.shape["mem"], mesh.shape["patch"]

    def on_device(ens, obs_pert, obs_innov, obs_pos, obs_prec):
        slabs, mloc, levels, width = ens.shape
        members, nob = obs_pert.shape[1:]
        group = width // n
        DMA = pltpu.SemaphoreType.DMA
        return pl.pallas_call(
            functools.partial(kernel, n, patches),
            out_shape=pltpu.VMEM(ens.shape, ens.dtype),
            in_specs=[pl.BlockSpec(memory_space=pltpu.HBM)] * 5,
            out_specs=pl.BlockSpec(memory_space=pltpu.VMEM),
            scratch_shapes=[
                pltpu.VMEM((slabs, members, levels, group), BF16),
                pltpu.VMEM((slabs, members, levels, group), BF16),
                pltpu.VMEM((slabs, members, nob), BF16),
                pltpu.VMEM((2, slabs, members, nob), BF16),
                pltpu.VMEM((3, slabs, nob), BF16),
                pltpu.VMEM((2, 3, slabs, nob), BF16),
                pltpu.VMEM((slabs, members, members), F32),
                pltpu.VMEM((slabs, 16, members), F32),
                pltpu.VMEM((members * levels, group), F32),
                pltpu.VMEM((members, levels * group), BF16),
                pltpu.VMEM((members, members), BF16),
                DMA((5,)), DMA((slabs,)),
                DMA((slabs,)), DMA((slabs,)), DMA((slabs,)), DMA((slabs,)), DMA((slabs,)),
                DMA((2, slabs)), DMA((2, slabs)), DMA((2,)), DMA((2,)),
                DMA((2, slabs)), DMA((2, slabs)), pltpu.SemaphoreType.REGULAR((2,)),
            ],
            compiler_params=pltpu.CompilerParams(
                collective_id=0, has_side_effects=True, vmem_limit_bytes=50000000),
        )(*[pltpu.with_memory_space_constraint(a, pltpu.HBM) for a in (ens, obs_pert, obs_innov, obs_pos, obs_prec)])

    placed = (
        P(None, "mem", None, "patch"),
        P(None, None, "patch"),
        P(None, "patch"),
        P(None, "patch"),
        P(None, "patch"),
    )
    return jax.shard_map(
        on_device,
        mesh=mesh,
        in_specs=placed,
        out_specs=P(None, "mem", None, "patch"),
        check_vma=False,
    )
```

```python
import functools
import jax
import jax.numpy as jnp
from jax import lax
from jax.experimental import pallas as pl
from jax.experimental.pallas import tpu as pltpu
from jax.sharding import PartitionSpec as P

loc_scale = 0.5
MESH = pl.DeviceIdType.MESH
F32 = jnp.float32
BF16 = jnp.bfloat16
NT = (((1,), (1,)), ((), ()))


def split(x):
    high = x.astype(BF16)
    return high, (x - high.astype(F32)).astype(BF16)


def mm(a, b):
    return jnp.dot(a, b, preferred_element_type=F32)


def mm3(a, b):
    return mm(a[0], b[0]) + (mm(a[0], b[1]) + mm(a[1], b[0]))


def peer_of(me, step, count):
    if count & (count - 1):
        return lax.rem(me + step, count)
    bit, peer = 1, 0
    while bit < count:
        mine = lax.rem(me // bit, 2)
        peer = peer + bit * ((1 - mine) if step & bit else mine)
        bit *= 2
    return peer


def kernel(
    n, patches, ens, pert, innov, pos, prec, out,
    xin, ybuf, own, near, small, small_near, gram, rhs, anom, abf, wide,
    local_sem, keep_sem, in_send, in_recv, out_send, out_recv, back_sem,
    z_send, z_recv, s_send, s_recv, f_send, f_recv, ready,
):
    slabs, mloc, levels, _ = ens.shape
    members, nob = pert.shape[1], pert.shape[2]
    group = ens.shape[3] // n
    half = nob // 2
    me = lax.axis_index("mem")
    patch = lax.axis_index("patch")
    core = lax.rem(me, 2)
    partner = me + 1 - 2 * core
    up = lax.rem(patch + 1, patches)
    down = lax.rem(patch + patches - 1, patches)
    steps = sorted(range(1, n), key=lambda d: (d < 2, d % 2, bin(d // 2).count("1"), d))
    peers = [peer_of(me, d, n) for d in steps]

    barrier = pltpu.get_barrier_semaphore()
    for q in peers:
        pl.semaphore_signal(barrier, inc=1, device_id=(q, patch), device_id_type=MESH)
    for z in (up, down):
        @pl.when(z > patch)
        def _():
            pl.semaphore_signal(barrier, inc=1, device_id=(me, z), device_id_type=MESH)

    load_pert = pltpu.make_async_copy(pert, own, local_sem.at[1])
    load_small = [
        pltpu.make_async_copy(ref, small.at[i], local_sem.at[2 + i])
        for i, ref in enumerate((innov, pos, prec))
    ]
    for c in load_small:
        c.start()

    def rows(q):
        return pl.ds(pl.multiple_of(q * mloc, mloc), mloc)

    def cols(q):
        return pl.ds(pl.multiple_of(q * group, group), group)

    keep = []
    for s in range(slabs):
        c = pltpu.make_async_copy(ens.at[s, :, :, cols(me)], xin.at[s, rows(me)], keep_sem.at[s])
        keep.append(c)

    lower = (up < patch).astype(jnp.int32) + (down < patch).astype(jnp.int32)
    pl.semaphore_wait(barrier, len(peers) + lower)

    mine = pl.ds(pl.multiple_of(core * half, half), half)
    theirs = pl.ds(pl.multiple_of((1 - core) * half, half), half)
    sends = []
    small_copies = []
    zc = {}
    targets = (up, down)

    def send_ens(s, some):
        for q in some:
            pltpu.make_async_remote_copy(
                ens.at[s, :, :, cols(q)], xin.at[s, rows(me)], in_send.at[s], in_recv.at[s],
                device_id=(q, patch), device_id_type=MESH).start()

    for d, z in enumerate(targets):
        @pl.when(z < patch)
        def _():
            pl.semaphore_signal(ready.at[1 - d], inc=1, device_id=(me, z), device_id_type=MESH)
    for d in (0, 1):
        small_copies.append(pltpu.make_async_remote_copy(
            small, small_near.at[d], s_send.at[d], s_recv.at[d],
            device_id=(me, targets[d]), device_id_type=MESH))
        for s in range(slabs):
            zc[d, s] = pltpu.make_async_remote_copy(
                pert.at[s, :, mine], near.at[d, s, :, mine], z_send.at[d, s], z_recv.at[d, s],
                device_id=(me, targets[d]), device_id_type=MESH)
            sends.append(zc[d, s])

    send_ens(0, peers)
    load_pert.start()
    for c in keep:
        c.start()
    for c in load_small:
        c.wait()
    for d, z in enumerate(targets):
        @pl.when(z < patch)
        def _():
            small_copies[d].start()
            zc[d, 0].start()
    for d, z in enumerate(targets):
        @pl.when(z > patch)
        def _():
            pl.semaphore_wait(ready.at[d], 1)
            small_copies[d].start()
            zc[d, 0].start()
    for s in range(1, slabs):
        for d in (0, 1):
            zc[d, s].start()
        send_ens(s, peers)

    load_pert.wait()
    center = (me.astype(F32) + 0.5) / n

    def accumulate(s, dev_ref, small_ref, offset, first, part=slice(None)):
        vals = small_ref[:, :, part].astype(F32)
        distance = vals[1] + offset - center
        taper = jnp.exp(-0.5 * (distance / loc_scale) ** 2)
        weight = taper * vals[2]
        dev = dev_ref[:, part]
        scaled = (dev.astype(F32) * weight[s:s + 1, :]).astype(BF16)
        row = jnp.broadcast_to(vals[0][s:s + 1, :], (16, vals.shape[2])).astype(BF16)
        both = lax.dot_general(
            jnp.concatenate([dev, row], axis=0), scaled, NT, preferred_element_type=F32)
        g, r = both[:members], both[members:]
        if first:
            gram[s] = g
            rhs[s] = r
        else:
            gram[s] += g
            rhs[s] += r

    for s in range(slabs):
        accumulate(s, own.at[s], small, 0.0, True)

    fwd = {}

    def relay(s):
        for d in (0, 1):
            zc[d, s].wait_recv()
            c = pltpu.make_async_remote_copy(
                near.at[d, s, :, mine], near.at[d, s, :, mine], f_send.at[d, s], f_recv.at[d, s],
                device_id=(partner, patch), device_id_type=MESH)
            c.start()
            fwd[d, s] = c

    def weights_of(s):
        diag = (
            lax.broadcasted_iota(jnp.int32, (members, members), 0)
            == lax.broadcasted_iota(jnp.int32, (members, members), 1)
        )
        system = gram[s] + jnp.where(diag, members - 1.0, 0.0)
        parts = split(system)
        fro2 = jnp.sum(jnp.sum(system * system, axis=0, keepdims=True), axis=1, keepdims=True)
        inv_fro = 1.0 / jnp.sqrt(fro2)
        cur = system * inv_fro
        cur2 = mm3(parts, parts) * (inv_fro * inv_fro)
        tail = 0.0625 * cur2 - 0.5625 * cur
        inverse = (
            jnp.where(diag, 2.25, 0.0) - 2.4375 * cur + 1.6875 * cur2
            + mm(cur2.astype(BF16), tail.astype(BF16))
        )
        inner = jnp.sum(inverse * rhs[s, 0:1, :], axis=1, keepdims=True)
        mean_weight = jnp.sum(inverse * inner, axis=0, keepdims=True) * inv_fro
        spread = inverse * jnp.sqrt((members - 1.0) * inv_fro)
        return (spread + mean_weight).astype(BF16)

    def centre(s):
        x = xin[s].astype(F32)
        average = jnp.sum(x, axis=0) * (1.0 / members)
        anom[...] = (x - average[None]).reshape(members * levels, group)
        for l in range(levels):
            abf[:, l * group:(l + 1) * group] = anom[pl.ds(l, members, stride=levels), :].astype(BF16)
        return average

    def apply(s, average, w):
        wide[...] = w
        parts = 1 if n & (n - 1) else 2
        size = members // parts
        for part in range(parts):
            block = (1 - part + (2 * part - 1) * (me // (n // 2))) if parts == 2 else 0
            base = pl.multiple_of(block * size, size)
            start = part * size * levels
            wp = wide[pl.ds(base, size), :]
            for l in range(0, levels, 2):
                mixed = mm(wp, abf[:, l * group:(l + 2) * group])
                anom[pl.ds(start + l, size, stride=levels), :] = mixed[:, :group]
                anom[pl.ds(start + l + 1, size, stride=levels), :] = mixed[:, group:]
            x = anom[pl.ds(start, size * levels), :].reshape(size, levels, group) + average[None]
            ybuf[s, pl.ds(base, size)] = x.astype(BF16)
            for d, q in zip(steps, peers):
                if parts == 1 or (d >= n // 2) == (part == 0):
                    pltpu.make_async_remote_copy(
                        ybuf.at[s, rows(q)], out.at[s, :, :, cols(me)], out_send.at[s],
                        out_recv.at[s], device_id=(q, patch), device_id_type=MESH).start()

    back = []
    others = (n - 1) * mloc

    def arrived(s):
        pltpu.make_async_copy(
            xin.at[s, pl.ds(0, others)], xin.at[s, pl.ds(0, others)], in_recv.at[s]).wait()

    for s in range(slabs):
        if s == 0:
            for c in small_copies:
                c.wait_recv()
        relay(s)
        for d, offset in ((0, -1.0), (1, 1.0)):
            accumulate(s, near.at[d, s], small_near.at[d], offset, False, mine)
        keep[s].wait()
        arrived(s)
        average = centre(s)
        for d, offset in ((0, -1.0), (1, 1.0)):
            fwd[d, s].wait_recv()
            accumulate(s, near.at[d, s], small_near.at[d], offset, False, theirs)
        w = weights_of(s)
        apply(s, average, w)
        c = pltpu.make_async_copy(ybuf.at[s, rows(me)], out.at[s, :, :, cols(me)], back_sem.at[s])
        c.start()
        back.append(c)

    for c in sends + small_copies:
        c.wait_send()
    for c in fwd.values():
        c.wait_send()
    for s in range(slabs):
        back[s].wait()
        for sem in (in_send, out_send, out_recv):
            pltpu.make_async_copy(
                xin.at[s, pl.ds(0, others)], xin.at[s, pl.ds(0, others)], sem.at[s]).wait()


def solution(mesh):
    n, patches = mesh.shape["mem"], mesh.shape["patch"]

    def on_device(ens, obs_pert, obs_innov, obs_pos, obs_prec):
        slabs, mloc, levels, width = ens.shape
        members, nob = obs_pert.shape[1:]
        group = width // n
        DMA = pltpu.SemaphoreType.DMA
        return pl.pallas_call(
            functools.partial(kernel, n, patches),
            out_shape=pltpu.VMEM(ens.shape, ens.dtype),
            in_specs=[pl.BlockSpec(memory_space=pltpu.HBM)] * 5,
            out_specs=pl.BlockSpec(memory_space=pltpu.VMEM),
            scratch_shapes=[
                pltpu.VMEM((slabs, members, levels, group), BF16),
                pltpu.VMEM((slabs, members, levels, group), BF16),
                pltpu.VMEM((slabs, members, nob), BF16),
                pltpu.VMEM((2, slabs, members, nob), BF16),
                pltpu.VMEM((3, slabs, nob), BF16),
                pltpu.VMEM((2, 3, slabs, nob), BF16),
                pltpu.VMEM((slabs, members, members), F32),
                pltpu.VMEM((slabs, 16, members), F32),
                pltpu.VMEM((members * levels, group), F32),
                pltpu.VMEM((members, levels * group), BF16),
                pltpu.VMEM((members, members), BF16),
                DMA((5,)), DMA((slabs,)),
                DMA((slabs,)), DMA((slabs,)), DMA((slabs,)), DMA((slabs,)), DMA((slabs,)),
                DMA((2, slabs)), DMA((2, slabs)), DMA((2,)), DMA((2,)),
                DMA((2, slabs)), DMA((2, slabs)), pltpu.SemaphoreType.REGULAR((2,)),
            ],
            compiler_params=pltpu.CompilerParams(
                collective_id=0, has_side_effects=True, vmem_limit_bytes=50000000),
        )(*[pltpu.with_memory_space_constraint(a, pltpu.HBM) for a in (ens, obs_pert, obs_innov, obs_pos, obs_prec)])

    placed = (
        P(None, "mem", None, "patch"),
        P(None, None, "patch"),
        P(None, "patch"),
        P(None, "patch"),
        P(None, "patch"),
    )
    return jax.shard_map(
        on_device,
        mesh=mesh,
        in_specs=placed,
        out_specs=P(None, "mem", None, "patch"),
        check_vma=False,
    )
```
